32 devices in a mesh: op: 8 (over y, x, core), tm: 4 (over z).
Axes of the slice: x: 2, y: 2, z: 4, core: 2. Of those that a mesh axis runs over, the one named last changes fastest.
Arguments:
- phi: bfloat16 [256, 32, 2, 128, 128], P('op', 'tm'), may hold values from -6 to 6
- tau_fwd: bfloat16 [2, 32, 2, 128, 128], P(None, 'tm'), may hold values from -0.375 to 0.375
- tau_bwd: bfloat16 [2, 32, 2, 128, 128], P(None, 'tm'), may hold values from -0.375 to 0.375
- src_times: int32 [2], replicated, may hold values from 0 to 31
- partner: int32 [256], replicated, may hold values from 0 to 255, each once
Outputs:
- corr: float32 [256, 2, 32, 2, 256], P('op', None, 'tm')
The draws below stay inside these ranges and needn't reach their ends.
Inputs may be any that keep to these rules, and one draw needn't show every extreme that they name: partner is a permutation of the operators. `src_times`: source times may repeat.
All inputs are finite; a program needn't handle non-finite values.
Results may differ from the reference program's by a relative error of at most 0.0041.
Values may be sent and summed in bfloat16 or wider, within the bound.
A program may use at most 256 MiB of HBM per device.

```python
import jax
import jax.numpy as jnp
from jax import lax

NV = 128
OPS = 256
NSRC = 2
NT = 32


def level_of(stream_key, shape, cuts, smallest, top_value):
    def one(dim, blocks):
        draws = jax.random.uniform(jax.random.fold_in(jax.random.fold_in(stream_key, 6), dim), (blocks,), jnp.float32, smallest / len(cuts), top_value / len(cuts))
        return jnp.repeat(jnp.exp(draws), shape[dim] // blocks).reshape((-1,) + (1,) * (len(shape) - dim - 1))

    gain = one(*cuts[0])
    for cut in cuts[1:]:
        gain = gain * one(*cut)
    return gain


def centred(rng, dims, scale, limit, pieces=(), kind=jnp.bfloat16):
    loudness = level_of(rng, dims, pieces, -0.22, 0.18) if pieces else 1.0
    values = jax.random.normal(rng, dims, jnp.float32) * scale * loudness
    return jnp.minimum(jnp.maximum(values, -limit), limit).astype(kind)


def setup_inputs(seed: int = 0) -> dict:
    keys = jax.random.split(jax.random.key(seed), 6)
    return {
        "phi": centred(keys[0], (OPS, NT, 2, NV, NV), 1.0, 6.0, ((0, 8), (1, 4))),
        "tau_fwd": centred(keys[1], (NSRC, NT, 2, NV, NV), (2 * NV) ** -0.5, 0.375, ((1, 4),)),
        "tau_bwd": centred(keys[2], (NSRC, NT, 2, NV, NV), (2 * NV) ** -0.5, 0.375, ((1, 4),)),
        "src_times": jax.random.randint(keys[3], (NSRC,), 0, NT).astype(jnp.int32),
        "partner": jax.random.permutation(keys[4], OPS).astype(jnp.int32),
    }


def rounded(value):
    low = lax.optimization_barrier(value.astype(jnp.bfloat16))
    return low.astype(jnp.float32)


def complex_product(spec, left_re, left_im, right_re, right_im):
    def inner(first, second):
        return jnp.einsum(spec, first, second)
    return inner(left_re, right_re) - inner(left_im, right_im), inner(left_re, right_im) + inner(left_im, right_re)


def reference(phi, tau_fwd, tau_bwd, src_times, partner):
    source = jnp.take(phi, src_times.astype(jnp.int32), axis=1).astype(jnp.float32)
    source_re = source[:, :, 0]
    source_im = source[:, :, 1]

    def one_time(when):
        fields = lax.dynamic_index_in_dim(phi, when, 1, False).astype(jnp.float32)
        fwd = lax.dynamic_index_in_dim(tau_fwd, when, 1, False).astype(jnp.float32)
        bwd = lax.dynamic_index_in_dim(tau_bwd, when, 1, False).astype(jnp.float32)
        left_re, left_im = complex_product("sab,jbc->jsac", fwd[:, 0], fwd[:, 1], fields[:, 0], fields[:, 1])
        left_re, left_im = rounded(left_re), rounded(left_im)
        sink_re, sink_im = complex_product("jsac,scd->jsad", left_re, left_im, bwd[:, 0], bwd[:, 1])
        sink_re, sink_im = rounded(sink_re), rounded(sink_im)
        real_part = jnp.einsum("jsad,ksad->jsk", sink_re, source_re) + jnp.einsum("jsad,ksad->jsk", sink_im, source_im)
        imag_part = jnp.einsum("jsad,ksad->jsk", sink_im, source_re) - jnp.einsum("jsad,ksad->jsk", sink_re, source_im)
        return jnp.stack([real_part, imag_part], 2) / NV

    result = lax.map(one_time, jnp.arange(NT, dtype=jnp.int32))
    result = jnp.transpose(result, (1, 2, 0, 3, 4))
    return jnp.take(result, partner.astype(jnp.int32), axis=4)
```

```python
import functools

import jax
import jax.numpy as jnp
from jax import lax
from jax.experimental import pallas as pl
from jax.experimental.pallas import tpu as pltpu
from jax.sharding import PartitionSpec as P

VMEM_LIMIT = 60 * 1024 * 1024


def sink_kernel(group, left_ref, phi_ref, right_ref, out_ref, wide):
    count = phi_ref.shape[0]
    width = phi_ref.shape[-1]
    for source in range(out_ref.shape[0]):
        left = left_ref[0, source]
        right = right_ref[0, source]

        @pl.loop(0, count // group)
        def _(step):
            start = step * group
            fields = [phi_ref[start + n, 0].reshape(2 * width, width) for n in range(group)]
            mid = jnp.dot(left, jnp.concatenate(fields, 1), preferred_element_type=jnp.float32)
            mid = mid.astype(jnp.bfloat16)
            rows = []
            for n in range(group):
                part = mid[:, n * width:(n + 1) * width]
                rows.append(jnp.concatenate([part[:width], part[width:]], 1))
            sink = jnp.dot(jnp.concatenate(rows, 0), right, preferred_element_type=jnp.float32)
            for n in range(group):
                base = pl.multiple_of((start + n) * width, width)
                for c in range(2):
                    wide[c, pl.ds(base, width), :] = sink[n * width:(n + 1) * width, c * width:(c + 1) * width]

        for c in range(2):

            @pl.loop(0, width, unroll=8)
            def _(row):
                picked = wide[c, pl.ds(row, count, stride=width), :]
                out_ref[source, c, 0, row] = picked.astype(jnp.bfloat16)


def sink_panels(left, phi, right):
    count, times, _, width, _ = phi.shape
    sources = left.shape[1]
    group = 4 if count % 4 == 0 else 1
    mults = 16 * count * times * sources * width ** 3
    return pl.pallas_call(
        functools.partial(sink_kernel, group),
        grid=(times,),
        in_specs=[
            pl.BlockSpec((1, sources, 2 * width, 2 * width), lambda t: (t, 0, 0, 0)),
            pl.BlockSpec((count, 1, 2, width, width), lambda t: (0, t, 0, 0, 0)),
            pl.BlockSpec((1, sources, 2 * width, 2 * width), lambda t: (t, 0, 0, 0)),
        ],
        out_specs=pl.BlockSpec((sources, 2, 1, width, count, width), lambda t: (0, 0, t, 0, 0, 0)),
        out_shape=jax.ShapeDtypeStruct((sources, 2, times, width, count, width), jnp.bfloat16),
        scratch_shapes=[pltpu.VMEM((2, count * width, width), jnp.float32)],
        compiler_params=pltpu.CompilerParams(vmem_limit_bytes=VMEM_LIMIT),
        cost_estimate=pl.CostEstimate(flops=2 * mults, bytes_accessed=6 * phi.size, transcendentals=0),
        name="sink_panels",
    )(left, phi, right)


def corr_kernel(panel_ref, source_ref, partner_ref, out_ref, total):
    step = pl.program_id(0)
    rows, width = panel_ref.shape[3], panel_ref.shape[5]
    half = out_ref.shape[1]
    wide = out_ref.shape[2]

    @pl.when(step == 0)
    def _():
        total[...] = jnp.zeros_like(total)

    panel = jnp.concatenate([panel_ref[0, :, :, r].reshape(2 * half, width) for r in range(rows)], 1)
    for c in range(2):
        source = jnp.concatenate([source_ref[:, 0, c, r].reshape(wide, width) for r in range(rows)], 1)
        total[c] += lax.dot_general(panel, source, (((1,), (1,)), ((), ())), preferred_element_type=jnp.float32)

    @pl.when(step == pl.num_programs(0) - 1)
    def _():
        place = lax.broadcasted_iota(jnp.int32, (wide, wide), 0)
        chosen = jnp.where(place == partner_ref[...], 1.0, 0.0).astype(jnp.float32)

        def permuted(value):
            return jnp.dot(value / width, chosen, precision=lax.Precision.HIGHEST, preferred_element_type=jnp.float32)

        out_ref[0] = permuted(total[0, :half] + total[1, half:])
        out_ref[1] = permuted(total[0, half:] - total[1, :half])


def correlate(panels, which, gathered, partner):
    _, _, times, width, count, _ = panels.shape
    ops, slabs, _, depth, local, _ = gathered.shape
    rows = 8
    per = depth // rows
    wide = ops * local
    flops = 2 * 4 * times * count * wide * width * width
    return pl.pallas_call(
        corr_kernel,
        grid=(slabs * per,),
        in_specs=[
            pl.BlockSpec((1, 2, times, rows, count, width), lambda g: (which, 0, 0, g, 0, 0)),
            pl.BlockSpec((ops, 1, 2, rows, local, width), lambda g: (0, g // per, 0, g % per, 0, 0)),
            pl.BlockSpec((1, wide), lambda g: (0, 0)),
        ],
        out_specs=pl.BlockSpec((2, times * count, wide), lambda g: (0, 0, 0)),
        out_shape=jax.ShapeDtypeStruct((2, times * count, wide), jnp.float32),
        scratch_shapes=[pltpu.VMEM((2, 2 * times * count, wide), jnp.float32)],
        compiler_params=pltpu.CompilerParams(vmem_limit_bytes=VMEM_LIMIT),
        cost_estimate=pl.CostEstimate(flops=flops, bytes_accessed=2 * panels.size, transcendentals=0),
        name="correlate",
    )(panels, gathered, partner)


def body(op, tm, phi, tau_fwd, tau_bwd, src_times, partner):
    count, times, _, width, _ = phi.shape
    sources = tau_fwd.shape[0]
    gathered = []
    for s in range(sources):
        when = src_times[s]
        local = lax.dynamic_index_in_dim(phi, when % times, 1, False)
        local = jnp.where(lax.axis_index("tm") == when // times, local, 0).astype(phi.dtype)
        piece = lax.psum_scatter(local, "tm", scatter_dimension=2, tiled=True)
        piece = jnp.transpose(piece, (1, 2, 0, 3))
        piece = lax.all_gather(piece, ("op", "tm"), axis=0, tiled=False)
        gathered.append(piece.reshape((op, tm) + piece.shape[1:]))

    f_re, f_im = tau_fwd[:, :, 0], tau_fwd[:, :, 1]
    b_re, b_im = tau_bwd[:, :, 0], tau_bwd[:, :, 1]
    left = jnp.concatenate([jnp.concatenate([f_re, -f_im], 3), jnp.concatenate([f_im, f_re], 3)], 2)
    right = jnp.concatenate([jnp.concatenate([b_re, b_im], 3), jnp.concatenate([-b_im, b_re], 3)], 2)
    panels = sink_panels(jnp.swapaxes(left, 0, 1), phi, jnp.swapaxes(right, 0, 1))

    parts = [correlate(panels, s, gathered[s], partner[None, :]) for s in range(sources)]
    corr = jnp.stack(parts, 0).reshape(sources, 2, times, count, -1)
    return jnp.transpose(corr, (3, 0, 2, 1, 4))


def solution(mesh):
    in_specs = (
        P("op", "tm", None, None, None),
        P(None, "tm", None, None, None),
        P(None, "tm", None, None, None),
        P(),
        P(),
    )
    out_specs = P("op", None, "tm", None, None)
    run = functools.partial(body, mesh.shape["op"], mesh.shape["tm"])
    return jax.shard_map(run, mesh=mesh, in_specs=in_specs, out_specs=out_specs, check_vma=False)
```
